32 devices in a mesh: slab: 8 (over z, y), mem: 4 (over x, core).
Axes of the slice: x: 2, y: 2, z: 4, core: 2. Of those that a mesh axis runs over, the one named last changes fastest.
Arguments:
- starting_states_set: float32 [128, 64, 1024], P('mem', 'slab'), may hold values from -6 to 6
- land_mask: int32 [64, 1024], P('slab'), may hold values 0 or 1
- cell_class: int32 [64, 1024], P('slab'), may hold values from 0 to 7
- kappa_table: float32 [8], replicated, may hold values from 0.08 to 0.2
- flow_table: float32 [2, 8], replicated, may hold values from -0.3 to 0.3
- obs_index: int32 [1024], P('slab'), may hold values from 0 to 8191
- obs_values: float32 [1024], P('slab'), may hold values from -24 to 24
- obs_var: float32 [1024], P('slab'), may hold values from 0.1 to 1
Outputs:
- analysis: float32 [128, 64, 1024], P('mem', 'slab')
The draws below stay inside these ranges and needn't reach their ends.
All inputs are finite; a program needn't handle non-finite values. No bound on the sum of `land_mask` on one device may be relied on, other than what follows from the above.
Results may differ from the reference program's by a relative error of at most 0.00016.
Values sent between devices are 32-bit elements; how exact they have to be, the bound alone decides.
A program may use at most 64 MiB of HBM per device.

```python
import math
import jax
import jax.numpy as jnp
from jax import lax

ENSEMBLE_SIZE = 128
EASTWARD_SPAN = 1024
LAT_DEV = 8
OBS_DEV = 128
STEPS = 8
ROOT_ITERATIONS = 8
NCLS = 8
NORTHWARD_SPAN = 64
NOBS = 1024
N_SLAB = 8


def plant(array, own_key, least, high):
    place = [jax.random.randint(jax.random.fold_in(own_key, axis), (), 0, length) for axis, length in enumerate(array.shape)]
    longest = array.shape.index(max(array.shape))
    neighbour = place[:longest] + [(place[longest] + 1) % array.shape[longest]] + place[longest + 1:]
    return array.at[tuple(place)].set(least).at[tuple(neighbour)].set(high)


def block_levels(rng, dims, split, smallest, top_value):
    level = 1.0
    for axis_at, parts in split:
        heights = jax.random.uniform(jax.random.fold_in(jax.random.fold_in(rng, 6), axis_at), (parts,), jnp.float32, smallest / len(split), top_value / len(split))
        level = level * jnp.repeat(jnp.exp(heights), dims[axis_at] // parts).reshape((-1,) + (1,) * (len(dims) - 1 - axis_at))
    return level


def noise(stream_key, shape, scale, bound, cuts=(), kind=jnp.bfloat16):
    result = jax.random.normal(stream_key, shape, jnp.float32) * scale
    if len(cuts) > 0:
        result = block_levels(stream_key, shape, cuts, -0.22, 0.18) * result
    return jnp.clip(result, min=-bound, max=bound).astype(kind)


def setup_inputs(seed: int = 0) -> dict:
    arg_keys = jax.random.split(jax.random.key(seed), 9)
    starting_states_set = noise(arg_keys[0], (ENSEMBLE_SIZE, NORTHWARD_SPAN, EASTWARD_SPAN), 1.0, 6.0, ((0, 4), (1, 8)), jnp.float32)
    land_mask = plant((jax.random.randint(arg_keys[1], (NORTHWARD_SPAN, EASTWARD_SPAN), 0, 8) < 7).astype(jnp.int32), jax.random.fold_in(arg_keys[1], 1), 0, 1)
    cell_class = plant(jax.random.randint(arg_keys[2], (NORTHWARD_SPAN, EASTWARD_SPAN), 0, NCLS), jax.random.fold_in(arg_keys[2], 1), 0, NCLS - 1).astype(jnp.int32)
    kappa_table = jnp.clip(jax.random.uniform(arg_keys[3], (NCLS,), jnp.float32, 0.08, 0.2), 0.08, 0.2)
    flow_table = jnp.clip(jax.random.uniform(arg_keys[4], (2, NCLS), jnp.float32, -0.3, 0.3), -0.3, 0.3)
    obs_index = plant(jax.random.randint(arg_keys[5], (NOBS,), 0, LAT_DEV * EASTWARD_SPAN), jax.random.fold_in(arg_keys[5], 1), 0, (LAT_DEV * EASTWARD_SPAN) - 1).astype(jnp.int32)
    obs_values = noise(arg_keys[6], (NOBS,), 4.0, 24.0, ((0, 8),), jnp.float32)
    obs_var = jnp.clip(jnp.exp(math.log(1.0) - 2.3025851 * jax.random.uniform(arg_keys[7], (NOBS,), jnp.float32) ** block_levels(arg_keys[7], (NOBS,), ((0, 8),), -0.2, 0.2)), 0.1, 1.0)
    return dict(starting_states_set=starting_states_set, land_mask=land_mask, cell_class=cell_class, kappa_table=kappa_table, flow_table=flow_table, obs_index=obs_index, obs_values=obs_values, obs_var=obs_var)


def advance(center, north, south, diffusion, flow_east, flow_north, wet_cells):
    edge = jnp.zeros_like(center[..., :1])
    east = jnp.concatenate([center[..., 1:], edge], axis=-1)
    west = jnp.concatenate([edge, center[..., :-1]], axis=-1)
    spread = north + south + east + west - 4.0 * center
    return wet_cells * (center + diffusion * spread - 0.5 * flow_east * (east - west) - 0.5 * flow_north * (north - south))

def reference(starting_states_set, land_mask, cell_class, kappa_table, flow_table, obs_index, obs_values, obs_var):
    highest = lax.Precision.HIGHEST
    diffusion = kappa_table[cell_class]
    flow_east = flow_table[0][cell_class]
    flow_north = flow_table[1][cell_class]
    wet_cells = land_mask.astype(jnp.float32)

    def single_prediction(current_profile):
        row_zero = jnp.zeros_like(current_profile[:1])
        for step in range(STEPS):
            north = jnp.concatenate([current_profile[1:], row_zero], axis=0)
            south = jnp.concatenate([row_zero, current_profile[:-1]], axis=0)
            current_profile = advance(current_profile, north, south, diffusion, flow_east, flow_north, wet_cells)
        return current_profile
    predictive_advance = lax.map(single_prediction, starting_states_set)
    raveled_vector = predictive_advance.reshape(ENSEMBLE_SIZE, NORTHWARD_SPAN * EASTWARD_SPAN)
    slab_of = jnp.arange(NOBS, dtype=jnp.int32) // OBS_DEV
    cells = slab_of * (LAT_DEV * EASTWARD_SPAN) + obs_index
    observed = jnp.take(raveled_vector, cells, axis=1)
    ybar = lax.optimization_barrier(jnp.sum(observed, axis=0)) / ENSEMBLE_SIZE
    factor = 1.0 + 2.0 * slab_of.astype(jnp.float32) / float(N_SLAB - 1)
    err = obs_var * factor
    anom = (observed - ybar) / jnp.sqrt(err * (ENSEMBLE_SIZE - 1.0))
    dev = (obs_values - ybar) / jnp.sqrt(err)
    gram = jnp.dot(anom, anom.T, precision=highest)
    proj = jnp.dot(anom, dev, precision=highest)
    ident = jnp.eye(ENSEMBLE_SIZE, dtype=jnp.float32)
    matrix = ident + gram
    scale = jnp.trace(matrix)
    upper = matrix / scale
    lower = ident
    for turn in range(ROOT_ITERATIONS):
        factor_q = 1.5 * ident - 0.5 * jnp.dot(lower, upper, precision=highest)
        upper = jnp.dot(upper, factor_q, precision=highest)
        lower = jnp.dot(factor_q, lower, precision=highest)
    transform_weights = lower / jnp.sqrt(scale)
    mean_w = jnp.dot(lower, jnp.dot(lower, proj, precision=highest), precision=highest) / (scale * jnp.sqrt(ENSEMBLE_SIZE - 1.0))
    total_w = transform_weights + mean_w[:, None]
    omega = 1.0 / ENSEMBLE_SIZE + total_w - (lax.optimization_barrier(jnp.sum(total_w, axis=0)) / ENSEMBLE_SIZE)[None, :]
    analysis = jnp.dot(omega.T, raveled_vector, precision=highest)
    return analysis.reshape(ENSEMBLE_SIZE, NORTHWARD_SPAN, EASTWARD_SPAN)
```

```python
import functools

import jax
import jax.numpy as jnp
from jax import lax
from jax.experimental import pallas as pl
from jax.experimental.pallas import tpu as pltpu
from jax.sharding import PartitionSpec as P

STEPS = 8
ROOT_ITERATIONS = 8
NCLS = 8
CHUNKS = 4


def halves(x):
    high = x.astype(jnp.bfloat16)
    return high, (x - high.astype(jnp.float32)).astype(jnp.bfloat16)


def left_parts(x):
    high, low = halves(x)
    return jnp.concatenate([high, high, low], axis=1)


def right_parts(x):
    high, low = halves(x)
    return jnp.concatenate([high, low, high], axis=0)


def product(left, right):
    return jnp.dot(left, right, preferred_element_type=jnp.float32)


def dot(a, b):
    return product(left_parts(a), right_parts(b))


def cycle_kernel(
    n_slab, n_mem,
    states, geo, kappa, flow, obs_index, obs_values, obs_var,
    out,
    buf, coef, geos, fore, mixed, gpart, grecv, gsum, precv, gfull,
    geo_send, geo_recv, y_send, y_recv, d_send, r_send, z_recv, keep_sem,
    a_send, a_recv, s_send, s_recv, p_send, p_recv, g_send, g_recv, b_send, b_recv,
):
    s = lax.axis_index("slab")
    m = lax.axis_index("mem")
    q, y = lax.div(s, 2), lax.rem(s, 2)
    n_pair, n_group = n_slab // 2, 2 * n_mem
    octs, rows, _, lon = states.shape[0] // 2, states.shape[1], states.shape[2], states.shape[3]
    span = lon // n_mem
    ens = fore.shape[1]
    block = ens // n_group
    kd = octs * 16
    group = y * n_mem + m
    last = n_pair - 1
    step_pair = 2 * y - 1

    def device(pair, side, member):
        return (2 * pair + side, member)

    def remote(src, dst, send, recv, where):
        return pltpu.make_async_remote_copy(
            src_ref=src, dst_ref=dst, send_sem=send, recv_sem=recv,
            device_id=where, device_id_type=pl.DeviceIdType.MESH,
        )

    def peer(k):
        other = lax.rem(group + k, n_group)
        return other, lax.div(other, n_mem), lax.rem(other, n_mem)

    barrier = pltpu.get_barrier_semaphore()
    for k in range(1, n_group):
        _, ty, tm = peer(k)
        pl.semaphore_signal(barrier, inc=1, device_id=device(q, ty, tm), device_id_type=pl.DeviceIdType.MESH)
    for k in range(1, n_pair):
        tq = lax.rem(q + k, n_pair)
        for side in range(2):
            pl.semaphore_signal(barrier, inc=1, device_id=device(tq, side, m), device_id_type=pl.DeviceIdType.MESH)
    pl.semaphore_wait(barrier, n_group - 1 + 2 * (n_pair - 1))

    def y_copy(c):
        return remote(
            states.at[octs * (1 - y) + c], buf.at[0, c, pl.ds(8 + 8 * y, 8)],
            y_send.at[c], y_recv.at[c], device(q, 1 - y, m),
        )

    def y_wait(c):
        return remote(
            states.at[c], buf.at[0, c, pl.ds(16 - 8 * y, 8)],
            y_send.at[c], y_recv.at[c], device(q, 1 - y, m),
        )

    def direct_copy(c):
        return remote(
            states.at[octs * y + c], buf.at[0, c, pl.ds(24 * (1 - y), 8)],
            d_send.at[c], z_recv.at[1 - y, c], device(q + step_pair, y, m),
        )

    def relay_copy(c):
        return remote(
            buf.at[0, c, pl.ds(16 - 8 * y, 8)], buf.at[0, c, pl.ds(24 * y, 8)],
            r_send.at[c], z_recv.at[y, c], device(q - step_pair, y, m),
        )

    def z_wait(side, c):
        return remote(
            states.at[c], buf.at[0, c, pl.ds(24 * side, 8)],
            d_send.at[c], z_recv.at[side, c], device(q, 1 - y, m),
        )

    def geo_pair():
        return remote(geo, geos.at[1 + y], geo_send.at[0], geo_recv.at[1 + y], device(q, 1 - y, m))

    def geo_side(side):
        return remote(
            geo, geos.at[3 * (1 - y)], geo_send.at[1 + side], geo_recv.at[3 * (1 - y)],
            device(q + step_pair, side, m),
        )

    def geo_wait(slot):
        return remote(geo, geos.at[slot], geo_send.at[0], geo_recv.at[slot], device(q, 1 - y, m))

    def keep(c):
        return pltpu.make_async_copy(states.at[octs * y + c], buf.at[0, c, pl.ds(8 + 8 * y, 8)], keep_sem.at[c])

    forward_edge = (q + step_pair >= 0) & (q + step_pair <= last)
    backward_edge = (q - step_pair >= 0) & (q - step_pair <= last)

    geo_pair().start()
    for c in range(octs):
        y_copy(c).start()

    @pl.when(forward_edge)
    def _():
        for side in range(2):
            geo_side(side).start()
        for c in range(octs):
            direct_copy(c).start()

    for c in range(octs):
        keep(c).start()
    geos[1 + y] = geo[...]

    @pl.when(q == 0)
    def _():
        geos[0] = jnp.zeros(geos.shape[1:], jnp.int32)
        for c in range(octs):
            buf[0, c, 0:8] = jnp.zeros((8, 8, lon), jnp.float32)

    @pl.when(q == last)
    def _():
        geos[3] = jnp.zeros(geos.shape[1:], jnp.int32)
        for c in range(octs):
            buf[0, c, 24:32] = jnp.zeros((8, 8, lon), jnp.float32)

    for c in range(octs):
        y_wait(c).wait_recv()

        @pl.when(backward_edge)
        def _():
            relay_copy(c).start()

    geo_wait(2 - y).wait_recv()

    @pl.when(q > 0)
    def _():
        geo_wait(0).wait_recv()

    @pl.when(q < last)
    def _():
        geo_wait(3).wait_recv()

    lane = lax.broadcasted_iota(jnp.int32, (8, lon), 1)

    def coefficients(k, carry):
        classes = geos[k, 0]
        wet = geos[k, 1].astype(jnp.float32)
        diffusion = jnp.zeros(classes.shape, jnp.float32)
        east = jnp.zeros(classes.shape, jnp.float32)
        north = jnp.zeros(classes.shape, jnp.float32)
        for label in range(NCLS):
            hit = classes == label
            diffusion = jnp.where(hit, kappa[label], diffusion)
            east = jnp.where(hit, flow[0, label], east)
            north = jnp.where(hit, flow[1, label], north)
        terms = (
            wet * (1.0 - 4.0 * diffusion),
            wet * (diffusion - 0.5 * north),
            wet * (diffusion + 0.5 * north),
            jnp.where(lane == lon - 1, 0.0, wet * (diffusion - 0.5 * east)),
            jnp.where(lane == 0, 0.0, wet * (diffusion + 0.5 * east)),
        )
        for index, term in enumerate(terms):
            for row in range(8):
                coef[8 * k + row, index] = jnp.broadcast_to(term[row : row + 1], (8, lon))
        return carry

    lax.fori_loop(0, 4, coefficients, 0)

    def a_copy(c, other, ty, tm):
        return remote(
            buf.at[0, c, pl.ds(8 + 8 * ty, 8), :, pl.ds(pl.multiple_of(span * tm, 128), span)],
            fore.at[:, pl.ds(pl.multiple_of(kd * m + 8 * octs * y + 8 * c, 8), 8), :],
            a_send.at[other, c], a_recv.at[group, c], device(q, ty, tm),
        )

    def a_wait(c, other, ty, tm):
        return remote(
            buf.at[0, c, pl.ds(8, 8), :, pl.ds(0, span)],
            fore.at[:, pl.ds(pl.multiple_of(kd * tm + 8 * octs * ty + 8 * c, 8), 8), :],
            a_send.at[other, c], a_recv.at[other, c], device(q, ty, tm),
        )

    def a_keep(c):
        return pltpu.make_async_copy(
            buf.at[0, c, pl.ds(8 + 8 * y, 8), :, pl.ds(pl.multiple_of(span * m, 128), span)],
            fore.at[:, pl.ds(pl.multiple_of(kd * m + 8 * octs * y + 8 * c, 8), 8), :],
            a_send.at[group, c],
        )

    for c in range(octs):
        keep(c).wait()

        @pl.when(q > 0)
        def _():
            z_wait(0, c).wait_recv()

        @pl.when(q < last)
        def _():
            z_wait(1, c).wait_recv()

        @pl.when(backward_edge)
        def _():
            relay_copy(c).wait_send()

        def two_steps(pair_step, carry):
            for parity in range(2):
                t = 2 * pair_step + parity

                def advance(r, inner):
                    center = buf[parity, c, r]
                    east = pltpu.roll(center, lon - 1, 1)
                    west = pltpu.roll(center, 1, 1)
                    buf[1 - parity, c, r] = (
                        coef[r, 0] * center
                        + coef[r, 1] * buf[parity, c, r + 1]
                        + coef[r, 2] * buf[parity, c, r - 1]
                        + coef[r, 3] * east
                        + coef[r, 4] * west
                    )
                    return inner

                lax.fori_loop(t + 1, 31 - t, advance, 0)
            return carry

        lax.fori_loop(0, STEPS // 2, two_steps, 0)
        for k in range(1, n_group):
            a_copy(c, *peer(k)).start()
        a_keep(c).start()

    for c in range(octs):
        a_keep(c).wait()
        for k in range(1, n_group):
            a_wait(c, *peer(k)).wait_recv()

    place = obs_index[...]
    n_obs = place.shape[1]
    hx = jnp.zeros((ens, n_obs), jnp.float32)
    inner = lax.broadcasted_iota(jnp.int32, (span, n_obs), 0) + span * m
    for row in range(rows):
        pick = jnp.where(inner + row * lon == place, 1.0, 0.0).astype(jnp.bfloat16)
        rest = fore[row]
        for _ in range(3):
            part = rest.astype(jnp.bfloat16)
            hx = hx + jnp.dot(part, pick, preferred_element_type=jnp.float32)
            rest = rest - part.astype(jnp.float32)
    column = place & (lon - 1)
    mine = (column >= span * m) & (column < span * m + span)
    ybar = jnp.sum(hx, axis=0, keepdims=True) / ens
    err = obs_var[...] * (1.0 + 2.0 * s.astype(jnp.float32) / float(n_slab - 1))
    anom = jnp.where(mine, (hx - ybar) / jnp.sqrt(err * (ens - 1.0)), 0.0)
    dev = (obs_values[...] - ybar) / jnp.sqrt(err)
    both = jnp.concatenate([anom, jnp.broadcast_to(dev, (ens, n_obs))], axis=0)
    high, low = halves(both)
    gpart[...] = lax.dot_general(
        left_parts(anom), jnp.concatenate([high, low, high], axis=1), (((1,), (1,)), ((), ())),
        preferred_element_type=jnp.float32,
    )

    def s_copy(other, ty, tm):
        return remote(
            gpart.at[pl.ds(pl.multiple_of(block * other, 8), block)], grecv.at[group],
            s_send.at[other], s_recv.at[group], device(q, ty, tm),
        )

    def s_wait(other, ty, tm):
        return remote(
            gpart.at[pl.ds(0, block)], grecv.at[other],
            s_send.at[other], s_recv.at[other], device(q, ty, tm),
        )

    for k in range(1, n_group):
        s_copy(*peer(k)).start()
    grecv[group] = gpart[pl.ds(pl.multiple_of(block * group, 8), block)]
    for k in range(1, n_group):
        s_wait(*peer(k)).wait_recv()
    total = grecv[0]
    for k in range(1, n_group):
        total = total + grecv[k]
    gsum[...] = total

    def p_copy(k):
        tq = lax.rem(q + k, n_pair)
        return remote(gsum, precv.at[q], p_send.at[tq], p_recv.at[q], device(tq, y, m))

    def p_wait(k):
        tq = lax.rem(q + k, n_pair)
        return remote(gsum, precv.at[tq], p_send.at[tq], p_recv.at[tq], device(tq, y, m))

    for k in range(1, n_pair):
        p_copy(k).start()
    precv[q] = total
    for k in range(1, n_pair):
        p_wait(k).wait_recv()
    total = precv[0]
    for k in range(1, n_pair):
        total = total + precv[k]
    own = pl.ds(pl.multiple_of(block * group, 8), block)
    gfull[own] = total

    def g_copy(other, ty, tm):
        return remote(gfull.at[own], gfull.at[own], g_send.at[other], g_recv.at[group], device(q, ty, tm))

    def g_wait(other, ty, tm):
        rows_there = gfull.at[pl.ds(pl.multiple_of(block * other, 8), block)]
        return remote(rows_there, rows_there, g_send.at[other], g_recv.at[other], device(q, ty, tm))

    for k in range(1, n_group):
        g_copy(*peer(k)).start()
    for k in range(1, n_group):
        g_wait(*peer(k)).wait_recv()

    ident = jnp.where(
        lax.broadcasted_iota(jnp.int32, (ens, ens), 0) == lax.broadcasted_iota(jnp.int32, (ens, ens), 1), 1.0, 0.0
    )
    matrix = ident + gfull[:, :ens]
    scale = jnp.sum(jnp.sum(matrix * ident, axis=1, keepdims=True), axis=0, keepdims=True)

    upper = matrix / scale
    factor = 1.5 * ident - 0.5 * upper
    upper, lower = dot(upper, factor), factor
    for _ in range(ROOT_ITERATIONS - 1):
        factor = 1.5 * ident - 0.5 * dot(lower, upper)
        upper, lower = dot(upper, factor), dot(factor, lower)
    mean_w = dot(lower, dot(lower, gfull[:, ens:])) / (scale * jnp.sqrt(jnp.float32(ens - 1.0)))
    total_w = lower / jnp.sqrt(scale) + mean_w
    omega = 1.0 / ens + total_w - jnp.sum(total_w, axis=0, keepdims=True) / ens
    turned = left_parts(omega.T)

    depth = rows // CHUNKS

    def b_copy(h, tm):
        return remote(
            mixed.at[pl.ds(depth * h, depth), pl.ds(pl.multiple_of(kd * tm, 8), kd)],
            out.at[pl.ds(depth * h, depth), :, pl.ds(pl.multiple_of(span * m, 128), span)],
            b_send.at[tm, h], b_recv.at[m, h], device(q, y, tm),
        )

    def b_wait(h, tm):
        return remote(
            mixed.at[pl.ds(depth * h, depth), pl.ds(0, kd)],
            out.at[pl.ds(depth * h, depth), :, pl.ds(pl.multiple_of(span * tm, 128), span)],
            b_send.at[tm, h], b_recv.at[tm, h], device(q, y, tm),
        )

    def b_keep(h):
        return pltpu.make_async_copy(
            mixed.at[pl.ds(depth * h, depth), pl.ds(pl.multiple_of(kd * m, 8), kd)],
            out.at[pl.ds(depth * h, depth), :, pl.ds(pl.multiple_of(span * m, 128), span)],
            b_send.at[m, h],
        )

    for h in range(CHUNKS):
        for row in range(depth * h, depth * h + depth):
            mixed[row] = product(turned, right_parts(fore[row]))
        for k in range(1, n_mem):
            b_copy(h, lax.rem(m + k, n_mem)).start()
        b_keep(h).start()

    geo_pair().wait_send()
    for c in range(octs):
        y_copy(c).wait_send()

    @pl.when(forward_edge)
    def _():
        for side in range(2):
            geo_side(side).wait_send()
        for c in range(octs):
            direct_copy(c).wait_send()

    for k in range(1, n_group):
        for c in range(octs):
            a_copy(c, *peer(k)).wait_send()
        s_copy(*peer(k)).wait_send()
        g_copy(*peer(k)).wait_send()
    for k in range(1, n_pair):
        p_copy(k).wait_send()
    for h in range(CHUNKS):
        b_keep(h).wait()
        for k in range(1, n_mem):
            b_copy(h, lax.rem(m + k, n_mem)).wait_send()
            b_wait(h, lax.rem(m + k, n_mem)).wait_recv()


def local(n_slab, n_mem, states, land_mask, cell_class, kappa, flow, obs_index, obs_values, obs_var):
    kd, rows, lon = states.shape
    ens = kd * n_mem
    n_pair, n_group, octs = n_slab // 2, 2 * n_mem, kd // 16
    span, block = lon // n_mem, ens // n_group
    n_obs = obs_index.shape[0]
    swapped = states.reshape(kd // 8, 8, rows, lon).transpose(0, 2, 1, 3)
    geo = jnp.stack([cell_class, land_mask])
    dma = pltpu.SemaphoreType.DMA
    vmem = pl.BlockSpec(memory_space=pltpu.VMEM)
    smem = pl.BlockSpec(memory_space=pltpu.SMEM)
    f32 = jnp.float32
    out = pl.pallas_call(
        functools.partial(cycle_kernel, n_slab, n_mem),
        out_shape=jax.ShapeDtypeStruct((rows, kd, lon), f32),
        in_specs=[vmem, vmem, smem, smem, vmem, vmem, vmem],
        out_specs=vmem,
        scratch_shapes=[
            pltpu.VMEM((2, octs, 4 * rows, 8, lon), f32),
            pltpu.VMEM((4 * rows, 5, 8, lon), f32),
            pltpu.VMEM((4, 2, rows, lon), jnp.int32),
            pltpu.VMEM((rows, ens, span), f32),
            pltpu.VMEM((rows, ens, span), f32),
            pltpu.VMEM((ens, 2 * ens), f32),
            pltpu.VMEM((n_group, block, 2 * ens), f32),
            pltpu.VMEM((block, 2 * ens), f32),
            pltpu.VMEM((n_pair, block, 2 * ens), f32),
            pltpu.VMEM((ens, 2 * ens), f32),
            dma((3,)), dma((4,)), dma((octs,)), dma((octs,)), dma((octs,)), dma((octs,)),
            dma((2, octs)), dma((octs,)),
            dma((n_group, octs)), dma((n_group, octs)),
            dma((n_group,)), dma((n_group,)), dma((n_pair,)), dma((n_pair,)),
            dma((n_group,)), dma((n_group,)), dma((n_mem, CHUNKS)), dma((n_mem, CHUNKS)),
        ],
        compiler_params=pltpu.CompilerParams(
            collective_id=0, has_side_effects=True, vmem_limit_bytes=40 * 1024 * 1024
        ),
        name="cycle",
    )(
        swapped, geo, kappa, flow,
        obs_index.reshape(1, n_obs), obs_values.reshape(1, n_obs), obs_var.reshape(1, n_obs),
    )
    return out.transpose(1, 0, 2)


def solution(mesh):
    return jax.shard_map(
        functools.partial(local, mesh.shape["slab"], mesh.shape["mem"]),
        mesh=mesh,
        in_specs=(
            P("mem", "slab", None),
            P("slab", None),
            P("slab", None),
            P(),
            P(),
            P("slab"),
            P("slab"),
            P("slab"),
        ),
        out_specs=P("mem", "slab", None),
        check_vma=False,
    )
```

```python
import functools

import jax
import jax.numpy as jnp
from jax import lax
from jax.experimental import pallas as pl
from jax.experimental.pallas import tpu as pltpu
from jax.sharding import PartitionSpec as P

STEPS = 8
ROOT_ITERATIONS = 8
NCLS = 8
CHUNKS = 4
HEIGHT = 4


def halves(x):
    high = x.astype(jnp.bfloat16)
    return high, (x - high.astype(jnp.float32)).astype(jnp.bfloat16)


def left_parts(x):
    high, low = halves(x)
    return jnp.concatenate([high, high, low], axis=1)


def right_parts(x):
    high, low = halves(x)
    return jnp.concatenate([high, low, high], axis=0)


def product(left, right):
    return jnp.dot(left, right, preferred_element_type=jnp.float32)


def dot(a, b):
    return product(left_parts(a), right_parts(b))


def cycle_kernel(
    n_slab, n_mem,
    states, geo, kappa, flow, obs_index, obs_values, obs_var,
    out,
    buf, coef, geos, fore, mixed, gpart, grecv, gsum, precv, gfull, turned,
    geo_send, geo_recv, y_send, y_recv, d_send, r_send, z_recv, keep_sem,
    a_send, a_recv, s_send, s_recv, p_send, p_recv, g_send, g_recv, b_send, b_recv,
):
    s = lax.axis_index("slab")
    m = lax.axis_index("mem")
    q, y = lax.div(s, 2), lax.rem(s, 2)
    n_pair, n_group = n_slab // 2, 2 * n_mem
    octs, rows, _, lon = states.shape[0] // 2, states.shape[1], states.shape[2], states.shape[3]
    span = lon // n_mem
    ens = fore.shape[2]
    n_line, line, core = n_mem // 2, lax.div(m, 2), lax.rem(m, 2)
    block = ens // n_group
    kd = octs * 16
    group = y * n_mem + m
    last = n_pair - 1
    step_pair = 2 * y - 1

    def quarter(member, j):
        return lax.rem(member, 2) * n_line + lax.rem(lax.div(member, 2) + j, n_line)

    def start_at(member, j):
        return pl.multiple_of(span * quarter(member, j), 128)

    def device(pair, side, member):
        return (2 * pair + side, member)

    def remote(src, dst, send, recv, where):
        return pltpu.make_async_remote_copy(
            src_ref=src, dst_ref=dst, send_sem=send, recv_sem=recv,
            device_id=where, device_id_type=pl.DeviceIdType.MESH,
        )

    def peer(k):
        other = lax.rem(group + k, n_group)
        return other, lax.div(other, n_mem), lax.rem(other, n_mem)

    barrier = pltpu.get_barrier_semaphore()
    for k in range(1, n_group):
        _, ty, tm = peer(k)
        pl.semaphore_signal(barrier, inc=1, device_id=device(q, ty, tm), device_id_type=pl.DeviceIdType.MESH)
    for k in range(1, n_pair):
        tq = lax.rem(q + k, n_pair)
        for side in range(2):
            pl.semaphore_signal(barrier, inc=1, device_id=device(tq, side, m), device_id_type=pl.DeviceIdType.MESH)
    pl.semaphore_wait(barrier, n_group - 1 + 2 * (n_pair - 1))

    def y_copy(c):
        return remote(
            states.at[octs * (1 - y) + c], buf.at[0, c, pl.ds(8 + 8 * y, 8)],
            y_send.at[c], y_recv.at[c], device(q, 1 - y, m),
        )

    def y_wait(c):
        return remote(
            states.at[c], buf.at[0, c, pl.ds(16 - 8 * y, 8)],
            y_send.at[c], y_recv.at[c], device(q, 1 - y, m),
        )

    def direct_copy(c):
        return remote(
            states.at[octs * y + c], buf.at[0, c, pl.ds(24 * (1 - y), 8)],
            d_send.at[c], z_recv.at[1 - y, c], device(q + step_pair, y, m),
        )

    def relay_copy(c):
        return remote(
            buf.at[0, c, pl.ds(16 - 8 * y, 8)], buf.at[0, c, pl.ds(24 * y, 8)],
            r_send.at[c], z_recv.at[y, c], device(q - step_pair, y, m),
        )

    def z_wait(side, c):
        return remote(
            states.at[c], buf.at[0, c, pl.ds(24 * side, 8)],
            d_send.at[c], z_recv.at[side, c], device(q, 1 - y, m),
        )

    def geo_pair():
        return remote(geo, geos.at[1 + y], geo_send.at[0], geo_recv.at[1 + y], device(q, 1 - y, m))

    def geo_side(side):
        return remote(
            geo, geos.at[3 * (1 - y)], geo_send.at[1 + side], geo_recv.at[3 * (1 - y)],
            device(q + step_pair, side, m),
        )

    def geo_wait(slot):
        return remote(geo, geos.at[slot], geo_send.at[0], geo_recv.at[slot], device(q, 1 - y, m))

    def keep(c):
        return pltpu.make_async_copy(states.at[octs * y + c], buf.at[0, c, pl.ds(8 + 8 * y, 8)], keep_sem.at[c])

    forward_edge = (q + step_pair >= 0) & (q + step_pair <= last)
    backward_edge = (q - step_pair >= 0) & (q - step_pair <= last)

    geo_pair().start()
    for c in range(octs):
        y_copy(c).start()

    @pl.when(forward_edge)
    def _():
        for side in range(2):
            geo_side(side).start()
        for c in range(octs):
            direct_copy(c).start()

    for c in range(octs):
        keep(c).start()
    geos[1 + y] = geo[...]

    @pl.when(q == 0)
    def _():
        geos[0] = jnp.zeros(geos.shape[1:], jnp.int32)
        for c in range(octs):
            buf[0, c, 0:8] = jnp.zeros((8, 8, lon), jnp.float32)

    @pl.when(q == last)
    def _():
        geos[3] = jnp.zeros(geos.shape[1:], jnp.int32)
        for c in range(octs):
            buf[0, c, 24:32] = jnp.zeros((8, 8, lon), jnp.float32)

    for c in range(octs):
        y_wait(c).wait_recv()

        @pl.when(backward_edge)
        def _():
            relay_copy(c).start()

    geo_wait(2 - y).wait_recv()

    @pl.when(q > 0)
    def _():
        geo_wait(0).wait_recv()

    @pl.when(q < last)
    def _():
        geo_wait(3).wait_recv()

    lane = lax.broadcasted_iota(jnp.int32, (8, lon), 1)

    def coefficients(k, carry):
        classes = geos[k, 0]
        wet = geos[k, 1].astype(jnp.float32)
        diffusion = jnp.zeros(classes.shape, jnp.float32)
        east = jnp.zeros(classes.shape, jnp.float32)
        north = jnp.zeros(classes.shape, jnp.float32)
        for label in range(NCLS):
            hit = classes == label
            diffusion = jnp.where(hit, kappa[label], diffusion)
            east = jnp.where(hit, flow[0, label], east)
            north = jnp.where(hit, flow[1, label], north)
        terms = (
            wet * (1.0 - 4.0 * diffusion),
            wet * (diffusion - 0.5 * north),
            wet * (diffusion + 0.5 * north),
            jnp.where(lane == lon - 1, 0.0, wet * (diffusion - 0.5 * east)),
            jnp.where(lane == 0, 0.0, wet * (diffusion + 0.5 * east)),
        )
        for index, term in enumerate(terms):
            for row in range(8):
                coef[8 * k + row, index] = jnp.broadcast_to(term[row : row + 1], (8, lon))
        return carry

    lax.fori_loop(0, 4, coefficients, 0)

    def a_copy(j, c, other, ty, tm):
        return remote(
            buf.at[0, c, pl.ds(8 + 8 * ty, 8), :, pl.ds(start_at(tm, j), span)],
            fore.at[j, :, pl.ds(pl.multiple_of(kd * m + 8 * octs * y + 8 * c, 8), 8), :],
            a_send.at[j, other, c], a_recv.at[j, group, c], device(q, ty, tm),
        )

    def a_wait(j, c, other, ty, tm):
        return remote(
            buf.at[0, c, pl.ds(8, 8), :, pl.ds(0, span)],
            fore.at[j, :, pl.ds(pl.multiple_of(kd * tm + 8 * octs * ty + 8 * c, 8), 8), :],
            a_send.at[j, other, c], a_recv.at[j, other, c], device(q, ty, tm),
        )

    def a_keep(j, c):
        return pltpu.make_async_copy(
            buf.at[0, c, pl.ds(8 + 8 * y, 8), :, pl.ds(start_at(m, j), span)],
            fore.at[j, :, pl.ds(pl.multiple_of(kd * m + 8 * octs * y + 8 * c, 8), 8), :],
            a_send.at[j, group, c],
        )

    def rest_start(c):
        for j in range(1, n_line):
            for k in range(1, n_group):
                a_copy(j, c, *peer(k)).start()
            a_keep(j, c).start()

    for c in range(octs):
        keep(c).wait()

        @pl.when(q > 0)
        def _():
            z_wait(0, c).wait_recv()

        @pl.when(q < last)
        def _():
            z_wait(1, c).wait_recv()

        @pl.when(backward_edge)
        def _():
            relay_copy(c).wait_send()

        def two_steps(pair_step, carry):
            for parity in range(2):
                t = 2 * pair_step + parity

                def advance(height, first, g):
                    base = first + height * g
                    level = [buf[parity, c, base - 1 + k] for k in range(height + 2)]
                    fresh = []
                    for k in range(height):
                        center = level[k + 1]
                        fresh.append(
                            coef[base + k, 0] * center
                            + coef[base + k, 1] * level[k + 2]
                            + coef[base + k, 2] * level[k]
                            + coef[base + k, 3] * pltpu.roll(center, lon - 1, 1)
                            + coef[base + k, 4] * pltpu.roll(center, 1, 1)
                        )
                    for k in range(height):
                        buf[1 - parity, c, base + k] = fresh[k]

                lax.fori_loop(0, (30 - 2 * t) // HEIGHT, lambda g, inner: (advance(HEIGHT, t + 1, g), inner)[1], 0)
                if HEIGHT == 4 and parity == 0:
                    advance(2, 29 - t, 0)
            return carry

        lax.fori_loop(0, STEPS // 2, two_steps, 0)
        for k in range(1, n_group):
            a_copy(0, c, *peer(k)).start()
        a_keep(0, c).start()
        rest_start(c)

    for c in range(octs):
        a_keep(0, c).wait()
        for k in range(1, n_group):
            a_wait(0, c, *peer(k)).wait_recv()

    place = obs_index[...]
    n_obs = place.shape[1]
    hx = jnp.zeros((ens, n_obs), jnp.float32)
    inner = lax.broadcasted_iota(jnp.int32, (span, n_obs), 0) + start_at(m, 0)
    for row in range(rows):
        pick = jnp.where(inner + row * lon == place, 1.0, 0.0).astype(jnp.bfloat16)
        rest = fore[0, row]
        for _ in range(3):
            part = rest.astype(jnp.bfloat16)
            hx = hx + jnp.dot(part, pick, preferred_element_type=jnp.float32)
            rest = rest - part.astype(jnp.float32)
    column = place & (lon - 1)
    mine = (column >= start_at(m, 0)) & (column < start_at(m, 0) + span)
    ybar = jnp.sum(hx, axis=0, keepdims=True) / ens
    err = obs_var[...] * (1.0 + 2.0 * s.astype(jnp.float32) / float(n_slab - 1))
    anom = jnp.where(mine, (hx - ybar) / jnp.sqrt(err * (ens - 1.0)), 0.0)
    dev = (obs_values[...] - ybar) / jnp.sqrt(err)
    both = jnp.concatenate([anom, jnp.broadcast_to(dev, (ens, n_obs))], axis=0)
    high, low = halves(both)
    gpart[...] = lax.dot_general(
        left_parts(anom), jnp.concatenate([high, low, high], axis=1), (((1,), (1,)), ((), ())),
        preferred_element_type=jnp.float32,
    )

    def s_copy(other, ty, tm):
        return remote(
            gpart.at[pl.ds(pl.multiple_of(block * other, 8), block)], grecv.at[group],
            s_send.at[other], s_recv.at[group], device(q, ty, tm),
        )

    def s_wait(other, ty, tm):
        return remote(
            gpart.at[pl.ds(0, block)], grecv.at[other],
            s_send.at[other], s_recv.at[other], device(q, ty, tm),
        )

    for k in range(1, n_group):
        s_copy(*peer(k)).start()
    grecv[group] = gpart[pl.ds(pl.multiple_of(block * group, 8), block)]
    for k in range(1, n_group):
        s_wait(*peer(k)).wait_recv()
    total = grecv[0]
    for k in range(1, n_group):
        total = total + grecv[k]
    gsum[...] = total

    def p_copy(k):
        tq = lax.rem(q + k, n_pair)
        return remote(gsum, precv.at[q], p_send.at[tq], p_recv.at[q], device(tq, y, m))

    def p_wait(k):
        tq = lax.rem(q + k, n_pair)
        return remote(gsum, precv.at[tq], p_send.at[tq], p_recv.at[tq], device(tq, y, m))

    for k in range(1, n_pair):
        p_copy(k).start()
    precv[q] = total
    for k in range(1, n_pair):
        p_wait(k).wait_recv()
    total = precv[0]
    for k in range(1, n_pair):
        total = total + precv[k]
    own = pl.ds(pl.multiple_of(block * group, 8), block)
    gfull[own] = total

    def g_copy(other, ty, tm):
        return remote(gfull.at[own], gfull.at[own], g_send.at[other], g_recv.at[group], device(q, ty, tm))

    def g_wait(other, ty, tm):
        rows_there = gfull.at[pl.ds(pl.multiple_of(block * other, 8), block)]
        return remote(rows_there, rows_there, g_send.at[other], g_recv.at[other], device(q, ty, tm))

    for k in range(1, n_group):
        g_copy(*peer(k)).start()
    for k in range(1, n_group):
        g_wait(*peer(k)).wait_recv()

    ident = jnp.where(
        lax.broadcasted_iota(jnp.int32, (ens, ens), 0) == lax.broadcasted_iota(jnp.int32, (ens, ens), 1), 1.0, 0.0
    )
    matrix = ident + gfull[:, :ens]
    scale = jnp.sum(jnp.sum(matrix * ident, axis=1, keepdims=True), axis=0, keepdims=True)

    upper = matrix / scale
    factor = 1.5 * ident - 0.5 * upper
    upper, lower = dot(upper, factor), factor
    for _ in range(ROOT_ITERATIONS - 1):
        factor = 1.5 * ident - 0.5 * dot(lower, upper)
        upper, lower = dot(upper, factor), dot(factor, lower)
    mean_w = dot(lower, dot(lower, gfull[:, ens:])) / (scale * jnp.sqrt(jnp.float32(ens - 1.0)))
    total_w = lower / jnp.sqrt(scale) + mean_w
    omega = 1.0 / ens + total_w - jnp.sum(total_w, axis=0, keepdims=True) / ens
    turned[...] = omega.T
    sibling = 2 * line + 1 - core
    weights = left_parts(
        jnp.concatenate(
            [turned[pl.ds(pl.multiple_of(kd * m, 8), kd)], turned[pl.ds(pl.multiple_of(kd * sibling, 8), kd)]], axis=0
        )
    )

    depth = rows // CHUNKS

    def b_copy(j, h):
        return remote(
            mixed.at[j, pl.ds(depth * h, depth)],
            out.at[pl.ds(depth * h, depth), :, pl.ds(start_at(m, j), span)],
            b_send.at[j, h], b_recv.at[j, h], device(q, y, sibling),
        )

    def b_wait(j, h):
        return remote(
            mixed.at[j, pl.ds(depth * h, depth)],
            out.at[pl.ds(depth * h, depth), :, pl.ds(start_at(sibling, j), span)],
            b_send.at[j, h], b_recv.at[j, h], device(q, y, sibling),
        )

    for j in range(n_line):
        if j > 0:
            for c in range(octs):
                a_keep(j, c).wait()
                for k in range(1, n_group):
                    a_wait(j, c, *peer(k)).wait_recv()
        for h in range(CHUNKS):
            for row in range(depth * h, depth * h + depth):
                result = product(weights, right_parts(fore[j, row]))
                mixed[j, row] = result[kd:]
                out[row, :, pl.ds(start_at(m, j), span)] = result[:kd]
            b_copy(j, h).start()

    geo_pair().wait_send()
    for c in range(octs):
        y_copy(c).wait_send()

    @pl.when(forward_edge)
    def _():
        for side in range(2):
            geo_side(side).wait_send()
        for c in range(octs):
            direct_copy(c).wait_send()

    for k in range(1, n_group):
        for c in range(octs):
            for j in range(n_line):
                a_copy(j, c, *peer(k)).wait_send()
        s_copy(*peer(k)).wait_send()
        g_copy(*peer(k)).wait_send()
    for k in range(1, n_pair):
        p_copy(k).wait_send()
    for j in range(n_line):
        for h in range(CHUNKS):
            b_copy(j, h).wait_send()
            b_wait(j, h).wait_recv()


def local(n_slab, n_mem, states, land_mask, cell_class, kappa, flow, obs_index, obs_values, obs_var):
    kd, rows, lon = states.shape
    ens = kd * n_mem
    n_pair, n_group, n_line, octs = n_slab // 2, 2 * n_mem, n_mem // 2, kd // 16
    span, block = lon // n_mem, ens // n_group
    n_obs = obs_index.shape[0]
    swapped = states.reshape(kd // 8, 8, rows, lon).transpose(0, 2, 1, 3)
    geo = jnp.stack([cell_class, land_mask])
    dma = pltpu.SemaphoreType.DMA
    vmem = pl.BlockSpec(memory_space=pltpu.VMEM)
    smem = pl.BlockSpec(memory_space=pltpu.SMEM)
    f32 = jnp.float32
    out = pl.pallas_call(
        functools.partial(cycle_kernel, n_slab, n_mem),
        out_shape=jax.ShapeDtypeStruct((rows, kd, lon), f32),
        in_specs=[vmem, vmem, smem, smem, vmem, vmem, vmem],
        out_specs=vmem,
        scratch_shapes=[
            pltpu.VMEM((2, octs, 4 * rows, 8, lon), f32),
            pltpu.VMEM((4 * rows, 5, 8, lon), f32),
            pltpu.VMEM((4, 2, rows, lon), jnp.int32),
            pltpu.VMEM((n_line, rows, ens, span), f32),
            pltpu.VMEM((n_line, rows, kd, span), f32),
            pltpu.VMEM((ens, 2 * ens), f32),
            pltpu.VMEM((n_group, block, 2 * ens), f32),
            pltpu.VMEM((block, 2 * ens), f32),
            pltpu.VMEM((n_pair, block, 2 * ens), f32),
            pltpu.VMEM((ens, 2 * ens), f32),
            pltpu.VMEM((ens, ens), f32),
            dma((3,)), dma((4,)), dma((octs,)), dma((octs,)), dma((octs,)), dma((octs,)),
            dma((2, octs)), dma((octs,)),
            dma((n_line, n_group, octs)), dma((n_line, n_group, octs)),
            dma((n_group,)), dma((n_group,)), dma((n_pair,)), dma((n_pair,)),
            dma((n_group,)), dma((n_group,)), dma((n_line, CHUNKS)), dma((n_line, CHUNKS)),
        ],
        compiler_params=pltpu.CompilerParams(
            collective_id=0, has_side_effects=True, vmem_limit_bytes=40 * 1024 * 1024
        ),
        name="cycle",
    )(
        swapped, geo, kappa, flow,
        obs_index.reshape(1, n_obs), obs_values.reshape(1, n_obs), obs_var.reshape(1, n_obs),
    )
    return out.transpose(1, 0, 2)


def solution(mesh):
    return jax.shard_map(
        functools.partial(local, mesh.shape["slab"], mesh.shape["mem"]),
        mesh=mesh,
        in_specs=(
            P("mem", "slab", None),
            P("slab", None),
            P("slab", None),
            P(),
            P(),
            P("slab"),
            P("slab"),
            P("slab"),
        ),
        out_specs=P("mem", "slab", None),
        check_vma=False,
    )
```

```python
import functools

import jax
import jax.numpy as jnp
from jax import lax
from jax.experimental import pallas as pl
from jax.experimental.pallas import tpu as pltpu
from jax.sharding import PartitionSpec as P

STEPS = 8
ROOT_ITERATIONS = 8
NCLS = 8
CHUNKS = 4
HEIGHT = 4
SPLIT = 2


def halves(x):
    high = x.astype(jnp.bfloat16)
    return high, (x - high.astype(jnp.float32)).astype(jnp.bfloat16)


def left_parts(x):
    high, low = halves(x)
    return jnp.concatenate([high, high, low], axis=1)


def right_parts(x):
    high, low = halves(x)
    return jnp.concatenate([high, low, high], axis=0)


def product(left, right):
    return jnp.dot(left, right, preferred_element_type=jnp.float32)


def dot(a, b):
    return product(left_parts(a), right_parts(b))


def cycle_kernel(
    n_slab, n_mem,
    states, classes_in, mask_in, kappa, flow, obs_index, obs_values, obs_var,
    out,
    buf, coef, geos, fore, mixed, gpart, grecv, gsum, precv, gfull, turned,
    geo_send, geo_recv, y_send, y_recv, d_send, r_send, z_recv, keep_sem,
    a_send, a_recv, s_send, s_recv, p_send, p_recv, g_send, g_recv, b_send, b_recv,
):
    s = lax.axis_index("slab")
    m = lax.axis_index("mem")
    q, y = lax.div(s, 2), lax.rem(s, 2)
    n_pair, n_group = n_slab // 2, 2 * n_mem
    octs, rows, _, lon = states.shape[0] // 2, states.shape[1], states.shape[2], states.shape[3]
    span = lon // n_mem
    ens = fore.shape[2]
    n_line, line, core = n_mem // 2, lax.div(m, 2), lax.rem(m, 2)
    block = ens // n_group
    kd = octs * 16
    group = y * n_mem + m
    last = n_pair - 1
    step_pair = 2 * y - 1

    def quarter(member, j):
        return lax.rem(member, 2) * n_line + lax.rem(lax.div(member, 2) + j, n_line)

    def start_at(member, j):
        return pl.multiple_of(span * quarter(member, j), 128)

    def device(pair, side, member):
        return (2 * pair + side, member)

    def remote(src, dst, send, recv, where):
        return pltpu.make_async_remote_copy(
            src_ref=src, dst_ref=dst, send_sem=send, recv_sem=recv,
            device_id=where, device_id_type=pl.DeviceIdType.MESH,
        )

    def peer(k):
        other = lax.rem(group + k, n_group)
        return other, lax.div(other, n_mem), lax.rem(other, n_mem)

    barrier = pltpu.get_barrier_semaphore()
    for k in range(1, n_group):
        _, ty, tm = peer(k)
        pl.semaphore_signal(barrier, inc=1, device_id=device(q, ty, tm), device_id_type=pl.DeviceIdType.MESH)
    for k in range(1, n_pair):
        tq = lax.rem(q + k, n_pair)
        for side in range(2):
            pl.semaphore_signal(barrier, inc=1, device_id=device(tq, side, m), device_id_type=pl.DeviceIdType.MESH)
    pl.semaphore_wait(barrier, n_group - 1 + 2 * (n_pair - 1))

    piece = 8 // SPLIT

    def y_copy(c, h):
        return remote(
            states.at[octs * (1 - y) + c, pl.ds(piece * h, piece)], buf.at[0, c, pl.ds(8 + 8 * y + piece * h, piece)],
            y_send.at[c, h], y_recv.at[c, h], device(q, 1 - y, m),
        )

    def y_wait(c, h):
        return remote(
            states.at[c, pl.ds(0, piece)], buf.at[0, c, pl.ds(16 - 8 * y + piece * h, piece)],
            y_send.at[c, h], y_recv.at[c, h], device(q, 1 - y, m),
        )

    def direct_copy(c, h):
        return remote(
            states.at[octs * y + c, pl.ds(piece * h, piece)], buf.at[0, c, pl.ds(24 * (1 - y) + piece * h, piece)],
            d_send.at[c, h], z_recv.at[1 - y, c, h], device(q + step_pair, y, m),
        )

    def relay_copy(c, h):
        return remote(
            buf.at[0, c, pl.ds(16 - 8 * y + piece * h, piece)], buf.at[0, c, pl.ds(24 * y + piece * h, piece)],
            r_send.at[c, h], z_recv.at[y, c, h], device(q - step_pair, y, m),
        )

    def z_wait(side, c, h):
        return remote(
            states.at[c, pl.ds(0, piece)], buf.at[0, c, pl.ds(24 * side + piece * h, piece)],
            d_send.at[c, h], z_recv.at[side, c, h], device(q, 1 - y, m),
        )

    fields = (classes_in, mask_in)

    def geo_pair(f):
        return remote(
            fields[f], geos.at[1 + y, f], geo_send.at[0, f], geo_recv.at[1 + y, f], device(q, 1 - y, m)
        )

    def geo_side(side, f):
        return remote(
            fields[f], geos.at[3 * (1 - y), f], geo_send.at[1 + side, f], geo_recv.at[3 * (1 - y), f],
            device(q + step_pair, side, m),
        )

    def geo_wait(slot, f):
        return remote(fields[f], geos.at[slot, f], geo_send.at[0, f], geo_recv.at[slot, f], device(q, 1 - y, m))

    def keep(c):
        return pltpu.make_async_copy(states.at[octs * y + c], buf.at[0, c, pl.ds(8 + 8 * y, 8)], keep_sem.at[c])

    forward_edge = (q + step_pair >= 0) & (q + step_pair <= last)
    backward_edge = (q - step_pair >= 0) & (q - step_pair <= last)

    for f in range(2):
        geo_pair(f).start()
    for c in range(octs):
        for h in range(SPLIT):
            y_copy(c, h).start()

    @pl.when(forward_edge)
    def _():
        for side in range(2):
            for f in range(2):
                geo_side(side, f).start()
        for c in range(octs):
            for h in range(SPLIT):
                direct_copy(c, h).start()

    for c in range(octs):
        keep(c).start()
    for f in range(2):
        geos[1 + y, f] = fields[f][...]

    @pl.when(q == 0)
    def _():
        geos[0] = jnp.zeros(geos.shape[1:], jnp.int32)
        for c in range(octs):
            buf[0, c, 0:8] = jnp.zeros((8, 8, lon), jnp.float32)

    @pl.when(q == last)
    def _():
        geos[3] = jnp.zeros(geos.shape[1:], jnp.int32)
        for c in range(octs):
            buf[0, c, 24:32] = jnp.zeros((8, 8, lon), jnp.float32)

    for c in range(octs):
        for h in range(SPLIT):
            y_wait(c, h).wait_recv()

            @pl.when(backward_edge)
            def _():
                relay_copy(c, h).start()

    for f in range(2):
        geo_wait(2 - y, f).wait_recv()

    @pl.when(q > 0)
    def _():
        for f in range(2):
            geo_wait(0, f).wait_recv()

    @pl.when(q < last)
    def _():
        for f in range(2):
            geo_wait(3, f).wait_recv()

    lane = lax.broadcasted_iota(jnp.int32, (8, lon), 1)

    def coefficients(k, carry):
        classes = geos[k, 0]
        wet = geos[k, 1].astype(jnp.float32)
        diffusion = jnp.zeros(classes.shape, jnp.float32)
        east = jnp.zeros(classes.shape, jnp.float32)
        north = jnp.zeros(classes.shape, jnp.float32)
        for label in range(NCLS):
            hit = classes == label
            diffusion = jnp.where(hit, kappa[label], diffusion)
            east = jnp.where(hit, flow[0, label], east)
            north = jnp.where(hit, flow[1, label], north)
        terms = (
            wet * (1.0 - 4.0 * diffusion),
            wet * (diffusion - 0.5 * north),
            wet * (diffusion + 0.5 * north),
            jnp.where(lane == lon - 1, 0.0, wet * (diffusion - 0.5 * east)),
            jnp.where(lane == 0, 0.0, wet * (diffusion + 0.5 * east)),
        )
        for index, term in enumerate(terms):
            for row in range(8):
                coef[8 * k + row, index] = jnp.broadcast_to(term[row : row + 1], (8, lon))
        return carry

    lax.fori_loop(0, 4, coefficients, 0)

    def a_copy(j, c, other, ty, tm):
        return remote(
            buf.at[0, c, pl.ds(8 + 8 * ty, 8), :, pl.ds(start_at(tm, j), span)],
            fore.at[j, :, pl.ds(pl.multiple_of(kd * m + 8 * octs * y + 8 * c, 8), 8), :],
            a_send.at[j, other, c], a_recv.at[j, group, c], device(q, ty, tm),
        )

    def a_wait(j, c, other, ty, tm):
        return remote(
            buf.at[0, c, pl.ds(8, 8), :, pl.ds(0, span)],
            fore.at[j, :, pl.ds(pl.multiple_of(kd * tm + 8 * octs * ty + 8 * c, 8), 8), :],
            a_send.at[j, other, c], a_recv.at[j, other, c], device(q, ty, tm),
        )

    def a_keep(j, c):
        return pltpu.make_async_copy(
            buf.at[0, c, pl.ds(8 + 8 * y, 8), :, pl.ds(start_at(m, j), span)],
            fore.at[j, :, pl.ds(pl.multiple_of(kd * m + 8 * octs * y + 8 * c, 8), 8), :],
            a_send.at[j, group, c],
        )

    def rest_start(c):
        for j in range(1, n_line):
            for k in range(1, n_group):
                a_copy(j, c, *peer(k)).start()
            a_keep(j, c).start()

    for c in range(octs):
        keep(c).wait()

        @pl.when(q > 0)
        def _():
            for h in range(SPLIT):
                z_wait(0, c, h).wait_recv()

        @pl.when(q < last)
        def _():
            for h in range(SPLIT):
                z_wait(1, c, h).wait_recv()

        @pl.when(backward_edge)
        def _():
            for h in range(SPLIT):
                relay_copy(c, h).wait_send()

        def two_steps(pair_step, carry):
            for parity in range(2):
                t = 2 * pair_step + parity

                def advance(height, first, g):
                    base = first + height * g
                    level = [buf[parity, c, base - 1 + k] for k in range(height + 2)]
                    fresh = []
                    for k in range(height):
                        center = level[k + 1]
                        fresh.append(
                            coef[base + k, 0] * center
                            + coef[base + k, 1] * level[k + 2]
                            + coef[base + k, 2] * level[k]
                            + coef[base + k, 3] * pltpu.roll(center, lon - 1, 1)
                            + coef[base + k, 4] * pltpu.roll(center, 1, 1)
                        )
                    for k in range(height):
                        buf[1 - parity, c, base + k] = fresh[k]

                lax.fori_loop(0, (30 - 2 * t) // HEIGHT, lambda g, inner: (advance(HEIGHT, t + 1, g), inner)[1], 0)
                if HEIGHT == 4 and parity == 0:
                    advance(2, 29 - t, 0)
            return carry

        lax.fori_loop(0, STEPS // 2, two_steps, 0)
        for k in range(1, n_group):
            a_copy(0, c, *peer(k)).start()
        a_keep(0, c).start()
        if c < octs - 1:
            rest_start(c)

    for c in range(octs):
        a_keep(0, c).wait()
        for k in range(1, n_group):
            a_wait(0, c, *peer(k)).wait_recv()

    place = obs_index[...]
    n_obs = place.shape[1]
    hx = jnp.zeros((ens, n_obs), jnp.float32)
    inner = lax.broadcasted_iota(jnp.int32, (span, n_obs), 0) + start_at(m, 0)
    for row in range(rows):
        pick = jnp.where(inner + row * lon == place, 1.0, 0.0).astype(jnp.bfloat16)
        rest = fore[0, row]
        for _ in range(3):
            part = rest.astype(jnp.bfloat16)
            hx = hx + jnp.dot(part, pick, preferred_element_type=jnp.float32)
            rest = rest - part.astype(jnp.float32)
    column = place & (lon - 1)
    mine = (column >= start_at(m, 0)) & (column < start_at(m, 0) + span)
    ybar = jnp.sum(hx, axis=0, keepdims=True) / ens
    err = obs_var[...] * (1.0 + 2.0 * s.astype(jnp.float32) / float(n_slab - 1))
    anom = jnp.where(mine, (hx - ybar) / jnp.sqrt(err * (ens - 1.0)), 0.0)
    dev = (obs_values[...] - ybar) / jnp.sqrt(err)
    both = jnp.concatenate([anom, jnp.broadcast_to(dev, (ens, n_obs))], axis=0)
    high, low = halves(both)
    gpart[...] = lax.dot_general(
        left_parts(anom), jnp.concatenate([high, low, high], axis=1), (((1,), (1,)), ((), ())),
        preferred_element_type=jnp.float32,
    )

    def s_copy(other, ty, tm):
        return remote(
            gpart.at[pl.ds(pl.multiple_of(block * other, 8), block)], grecv.at[group],
            s_send.at[other], s_recv.at[group], device(q, ty, tm),
        )

    def s_wait(other, ty, tm):
        return remote(
            gpart.at[pl.ds(0, block)], grecv.at[other],
            s_send.at[other], s_recv.at[other], device(q, ty, tm),
        )

    for k in range(1, n_group):
        s_copy(*peer(k)).start()
    rest_start(octs - 1)
    grecv[group] = gpart[pl.ds(pl.multiple_of(block * group, 8), block)]
    for k in range(1, n_group):
        s_wait(*peer(k)).wait_recv()
    total = grecv[0]
    for k in range(1, n_group):
        total = total + grecv[k]
    gsum[...] = total

    def p_copy(k):
        tq = lax.rem(q + k, n_pair)
        return remote(gsum, precv.at[q], p_send.at[tq], p_recv.at[q], device(tq, y, m))

    def p_wait(k):
        tq = lax.rem(q + k, n_pair)
        return remote(gsum, precv.at[tq], p_send.at[tq], p_recv.at[tq], device(tq, y, m))

    for k in range(1, n_pair):
        p_copy(k).start()
    precv[q] = total
    for k in range(1, n_pair):
        p_wait(k).wait_recv()
    total = precv[0]
    for k in range(1, n_pair):
        total = total + precv[k]
    own = pl.ds(pl.multiple_of(block * group, 8), block)
    gfull[own] = total

    def g_copy(other, ty, tm):
        return remote(gfull.at[own], gfull.at[own], g_send.at[other], g_recv.at[group], device(q, ty, tm))

    def g_wait(other, ty, tm):
        rows_there = gfull.at[pl.ds(pl.multiple_of(block * other, 8), block)]
        return remote(rows_there, rows_there, g_send.at[other], g_recv.at[other], device(q, ty, tm))

    for k in range(1, n_group):
        g_copy(*peer(k)).start()
    for k in range(1, n_group):
        g_wait(*peer(k)).wait_recv()

    ident = jnp.where(
        lax.broadcasted_iota(jnp.int32, (ens, ens), 0) == lax.broadcasted_iota(jnp.int32, (ens, ens), 1), 1.0, 0.0
    )
    matrix = ident + gfull[:, :ens]
    scale = jnp.sum(jnp.sum(matrix * ident, axis=1, keepdims=True), axis=0, keepdims=True)

    upper = matrix / scale
    factor = 1.5 * ident - 0.5 * upper
    upper, lower = dot(upper, factor), factor
    for _ in range(ROOT_ITERATIONS - 1):
        factor = 1.5 * ident - 0.5 * dot(lower, upper)
        upper, lower = dot(upper, factor), dot(factor, lower)
    mean_w = dot(lower, dot(lower, gfull[:, ens:])) / (scale * jnp.sqrt(jnp.float32(ens - 1.0)))
    total_w = lower / jnp.sqrt(scale) + mean_w
    omega = 1.0 / ens + total_w - jnp.sum(total_w, axis=0, keepdims=True) / ens
    turned[...] = omega.T
    sibling = 2 * line + 1 - core
    weights = left_parts(
        jnp.concatenate(
            [turned[pl.ds(pl.multiple_of(kd * m, 8), kd)], turned[pl.ds(pl.multiple_of(kd * sibling, 8), kd)]], axis=0
        )
    )

    depth = rows // CHUNKS

    def b_copy(j, h):
        return remote(
            mixed.at[j, pl.ds(depth * h, depth)],
            out.at[pl.ds(depth * h, depth), :, pl.ds(start_at(m, j), span)],
            b_send.at[j, h], b_recv.at[j, h], device(q, y, sibling),
        )

    def b_wait(j, h):
        return remote(
            mixed.at[j, pl.ds(depth * h, depth)],
            out.at[pl.ds(depth * h, depth), :, pl.ds(start_at(sibling, j), span)],
            b_send.at[j, h], b_recv.at[j, h], device(q, y, sibling),
        )

    for j in range(n_line):
        if j > 0:
            for c in range(octs):
                a_keep(j, c).wait()
                for k in range(1, n_group):
                    a_wait(j, c, *peer(k)).wait_recv()
        for h in range(CHUNKS):
            for row in range(depth * h, depth * h + depth):
                result = product(weights, right_parts(fore[j, row]))
                mixed[j, row] = result[kd:]
                out[row, :, pl.ds(start_at(m, j), span)] = result[:kd]
            b_copy(j, h).start()

    for f in range(2):
        geo_pair(f).wait_send()
    for c in range(octs):
        for h in range(SPLIT):
            y_copy(c, h).wait_send()

    @pl.when(forward_edge)
    def _():
        for side in range(2):
            for f in range(2):
                geo_side(side, f).wait_send()
        for c in range(octs):
            for h in range(SPLIT):
                direct_copy(c, h).wait_send()

    for k in range(1, n_group):
        for c in range(octs):
            for j in range(n_line):
                a_copy(j, c, *peer(k)).wait_send()
        s_copy(*peer(k)).wait_send()
        g_copy(*peer(k)).wait_send()
    for k in range(1, n_pair):
        p_copy(k).wait_send()
    for j in range(n_line):
        for h in range(CHUNKS):
            b_copy(j, h).wait_send()
            b_wait(j, h).wait_recv()


def local(n_slab, n_mem, states, land_mask, cell_class, kappa, flow, obs_index, obs_values, obs_var):
    kd, rows, lon = states.shape
    ens = kd * n_mem
    n_pair, n_group, n_line, octs = n_slab // 2, 2 * n_mem, n_mem // 2, kd // 16
    span, block = lon // n_mem, ens // n_group
    n_obs = obs_index.shape[0]
    swapped = states.reshape(kd // 8, 8, rows, lon).transpose(0, 2, 1, 3)
    dma = pltpu.SemaphoreType.DMA
    vmem = pl.BlockSpec(memory_space=pltpu.VMEM)
    smem = pl.BlockSpec(memory_space=pltpu.SMEM)
    f32 = jnp.float32
    out = pl.pallas_call(
        functools.partial(cycle_kernel, n_slab, n_mem),
        out_shape=jax.ShapeDtypeStruct((rows, kd, lon), f32),
        in_specs=[vmem, vmem, vmem, smem, smem, vmem, vmem, vmem],
        out_specs=vmem,
        scratch_shapes=[
            pltpu.VMEM((2, octs, 4 * rows, 8, lon), f32),
            pltpu.VMEM((4 * rows, 5, 8, lon), f32),
            pltpu.VMEM((4, 2, rows, lon), jnp.int32),
            pltpu.VMEM((n_line, rows, ens, span), f32),
            pltpu.VMEM((n_line, rows, kd, span), f32),
            pltpu.VMEM((ens, 2 * ens), f32),
            pltpu.VMEM((n_group, block, 2 * ens), f32),
            pltpu.VMEM((block, 2 * ens), f32),
            pltpu.VMEM((n_pair, block, 2 * ens), f32),
            pltpu.VMEM((ens, 2 * ens), f32),
            pltpu.VMEM((ens, ens), f32),
            dma((3, 2)), dma((4, 2)), dma((octs, SPLIT)), dma((octs, SPLIT)), dma((octs, SPLIT)), dma((octs, SPLIT)),
            dma((2, octs, SPLIT)), dma((octs,)),
            dma((n_line, n_group, octs)), dma((n_line, n_group, octs)),
            dma((n_group,)), dma((n_group,)), dma((n_pair,)), dma((n_pair,)),
            dma((n_group,)), dma((n_group,)), dma((n_line, CHUNKS)), dma((n_line, CHUNKS)),
        ],
        compiler_params=pltpu.CompilerParams(
            collective_id=0, has_side_effects=True, vmem_limit_bytes=40 * 1024 * 1024
        ),
        name="cycle",
    )(
        swapped, cell_class, land_mask, kappa, flow,
        obs_index.reshape(1, n_obs), obs_values.reshape(1, n_obs), obs_var.reshape(1, n_obs),
    )
    return out.transpose(1, 0, 2)


def solution(mesh):
    return jax.shard_map(
        functools.partial(local, mesh.shape["slab"], mesh.shape["mem"]),
        mesh=mesh,
        in_specs=(
            P("mem", "slab", None),
            P("slab", None),
            P("slab", None),
            P(),
            P(),
            P("slab"),
            P("slab"),
            P("slab"),
        ),
        out_specs=P("mem", "slab", None),
        check_vma=False,
    )
```

```python
import functools

import jax
import jax.numpy as jnp
from jax import lax
from jax.experimental import pallas as pl
from jax.experimental.pallas import tpu as pltpu
from jax.sharding import PartitionSpec as P

STEPS = 8
ROOT_ITERATIONS = 8
NCLS = 8
CHUNKS = 4
HEIGHT = 4
SPLIT = 2


def halves(x):
    high = x.astype(jnp.bfloat16)
    return high, (x - high.astype(jnp.float32)).astype(jnp.bfloat16)


def left_parts(x):
    high, low = halves(x)
    return jnp.concatenate([high, high, low], axis=1)


def right_parts(x):
    high, low = halves(x)
    return jnp.concatenate([high, low, high], axis=0)


def product(left, right):
    return jnp.dot(left, right, preferred_element_type=jnp.float32)


def dot(a, b):
    return product(left_parts(a), right_parts(b))


def cycle_kernel(
    n_slab, n_mem,
    states, classes_in, mask_in, kappa, flow, obs_index, obs_values, obs_var,
    out,
    buf, coef, geos, fore, mixed, gpart, grecv, gsum, precv, gfull, turned, ready,
    geo_send, geo_recv, y_send, y_recv, d_send, r_send, z_recv, keep_sem,
    a_send, a_recv, s_send, s_recv, p_send, p_recv, g_send, g_recv, b_send, b_recv,
):
    s = lax.axis_index("slab")
    m = lax.axis_index("mem")
    q, y = lax.div(s, 2), lax.rem(s, 2)
    n_pair, n_group = n_slab // 2, 2 * n_mem
    octs, rows, _, lon = states.shape[0] // 2, states.shape[1], states.shape[2], states.shape[3]
    span = lon // n_mem
    ens = fore.shape[2]
    n_line, line, core = n_mem // 2, lax.div(m, 2), lax.rem(m, 2)
    block = ens // n_group
    kd = octs * 16
    group = y * n_mem + m
    last = n_pair - 1
    step_pair = 2 * y - 1

    def quarter(member, j):
        return lax.rem(member, 2) * n_line + lax.rem(lax.div(member, 2) + j, n_line)

    def start_at(member, j):
        return pl.multiple_of(span * quarter(member, j), 128)

    def device(pair, side, member):
        return (2 * pair + side, member)

    def remote(src, dst, send, recv, where):
        return pltpu.make_async_remote_copy(
            src_ref=src, dst_ref=dst, send_sem=send, recv_sem=recv,
            device_id=where, device_id_type=pl.DeviceIdType.MESH,
        )

    def peer(k):
        other = lax.rem(group + k, n_group)
        return other, lax.div(other, n_mem), lax.rem(other, n_mem)

    barrier = pltpu.get_barrier_semaphore()
    for k in range(1, n_group):
        _, ty, tm = peer(k)
        pl.semaphore_signal(barrier, inc=1, device_id=device(q, ty, tm), device_id_type=pl.DeviceIdType.MESH)
    for k in range(1, n_pair):
        tq = lax.rem(q + k, n_pair)
        for side in range(2):
            pl.semaphore_signal(barrier, inc=1, device_id=device(tq, side, m), device_id_type=pl.DeviceIdType.MESH)
    pl.semaphore_wait(barrier, n_group - 1 + 2 * (n_pair - 1))

    piece = 8 // SPLIT

    def y_copy(c, h):
        return remote(
            states.at[octs * (1 - y) + c, pl.ds(piece * h, piece)], buf.at[0, c, pl.ds(8 + 8 * y + piece * h, piece)],
            y_send.at[c, h], y_recv.at[c, h], device(q, 1 - y, m),
        )

    def y_wait(c, h):
        return remote(
            states.at[c, pl.ds(0, piece)], buf.at[0, c, pl.ds(16 - 8 * y + piece * h, piece)],
            y_send.at[c, h], y_recv.at[c, h], device(q, 1 - y, m),
        )

    def direct_copy(c, h):
        return remote(
            states.at[octs * y + c, pl.ds(piece * h, piece)], buf.at[0, c, pl.ds(24 * (1 - y) + piece * h, piece)],
            d_send.at[c, h], z_recv.at[1 - y, c, h], device(q + step_pair, y, m),
        )

    def relay_copy(c, h):
        return remote(
            buf.at[0, c, pl.ds(16 - 8 * y + piece * h, piece)], buf.at[0, c, pl.ds(24 * y + piece * h, piece)],
            r_send.at[c, h], z_recv.at[y, c, h], device(q - step_pair, y, m),
        )

    def z_wait(side, c, h):
        return remote(
            states.at[c, pl.ds(0, piece)], buf.at[0, c, pl.ds(24 * side + piece * h, piece)],
            d_send.at[c, h], z_recv.at[side, c, h], device(q, 1 - y, m),
        )

    fields = (classes_in, mask_in)

    def geo_pair(f):
        return remote(
            fields[f], geos.at[1 + y, f], geo_send.at[0, f], geo_recv.at[1 + y, f], device(q, 1 - y, m)
        )

    def geo_side(side, f):
        return remote(
            fields[f], geos.at[3 * (1 - y), f], geo_send.at[1 + side, f], geo_recv.at[3 * (1 - y), f],
            device(q + step_pair, side, m),
        )

    def geo_wait(slot, f):
        return remote(fields[f], geos.at[slot, f], geo_send.at[0, f], geo_recv.at[slot, f], device(q, 1 - y, m))

    def keep(c):
        return pltpu.make_async_copy(states.at[octs * y + c], buf.at[0, c, pl.ds(8 + 8 * y, 8)], keep_sem.at[c])

    forward_edge = (q + step_pair >= 0) & (q + step_pair <= last)
    backward_edge = (q - step_pair >= 0) & (q - step_pair <= last)

    for f in range(2):
        geo_pair(f).start()
    for c in range(octs):
        for h in range(SPLIT):
            y_copy(c, h).start()

    @pl.when(forward_edge)
    def _():
        for side in range(2):
            for f in range(2):
                geo_side(side, f).start()
        for c in range(octs):
            for h in range(SPLIT):
                direct_copy(c, h).start()

    for c in range(octs):
        keep(c).start()
    for f in range(2):
        geos[1 + y, f] = fields[f][...]

    @pl.when(q == 0)
    def _():
        geos[0] = jnp.zeros(geos.shape[1:], jnp.int32)
        for c in range(octs):
            buf[0, c, 0:8] = jnp.zeros((8, 8, lon), jnp.float32)

    @pl.when(q == last)
    def _():
        geos[3] = jnp.zeros(geos.shape[1:], jnp.int32)
        for c in range(octs):
            buf[0, c, 24:32] = jnp.zeros((8, 8, lon), jnp.float32)

    for c in range(octs):
        for h in range(SPLIT):
            y_wait(c, h).wait_recv()

            @pl.when(backward_edge)
            def _():
                relay_copy(c, h).start()

    for f in range(2):
        geo_wait(2 - y, f).wait_recv()

    @pl.when(q > 0)
    def _():
        for f in range(2):
            geo_wait(0, f).wait_recv()

    @pl.when(q < last)
    def _():
        for f in range(2):
            geo_wait(3, f).wait_recv()

    lane = lax.broadcasted_iota(jnp.int32, (8, lon), 1)

    def coefficients(k, carry):
        classes = geos[k, 0]
        wet = geos[k, 1].astype(jnp.float32)
        diffusion = jnp.zeros(classes.shape, jnp.float32)
        east = jnp.zeros(classes.shape, jnp.float32)
        north = jnp.zeros(classes.shape, jnp.float32)
        for label in range(NCLS):
            hit = classes == label
            diffusion = jnp.where(hit, kappa[label], diffusion)
            east = jnp.where(hit, flow[0, label], east)
            north = jnp.where(hit, flow[1, label], north)
        terms = (
            wet * (1.0 - 4.0 * diffusion),
            wet * (diffusion - 0.5 * north),
            wet * (diffusion + 0.5 * north),
            jnp.where(lane == lon - 1, 0.0, wet * (diffusion - 0.5 * east)),
            jnp.where(lane == 0, 0.0, wet * (diffusion + 0.5 * east)),
        )
        for index, term in enumerate(terms):
            for row in range(8):
                coef[8 * k + row, index] = jnp.broadcast_to(term[row : row + 1], (8, lon))
        return carry

    lax.fori_loop(0, 4, coefficients, 0)

    def a_copy(j, c, other, ty, tm):
        return remote(
            buf.at[0, c, pl.ds(8 + 8 * ty, 8), :, pl.ds(start_at(tm, j), span)],
            fore.at[j, :, pl.ds(pl.multiple_of(kd * m + 8 * octs * y + 8 * c, 8), 8), :],
            a_send.at[j, other, c], a_recv.at[j, group, c], device(q, ty, tm),
        )

    def a_wait(j, c, other, ty, tm):
        return remote(
            buf.at[0, c, pl.ds(8, 8), :, pl.ds(0, span)],
            fore.at[j, :, pl.ds(pl.multiple_of(kd * tm + 8 * octs * ty + 8 * c, 8), 8), :],
            a_send.at[j, other, c], a_recv.at[j, other, c], device(q, ty, tm),
        )

    def a_keep(j, c):
        return pltpu.make_async_copy(
            buf.at[0, c, pl.ds(8 + 8 * y, 8), :, pl.ds(start_at(m, j), span)],
            fore.at[j, :, pl.ds(pl.multiple_of(kd * m + 8 * octs * y + 8 * c, 8), 8), :],
            a_send.at[j, group, c],
        )

    def rest_start(c):
        for j in range(1, n_line):
            for k in range(1, n_group):
                a_copy(j, c, *peer(k)).start()
            a_keep(j, c).start()

    for c in range(octs):
        keep(c).wait()

        @pl.when(q > 0)
        def _():
            for h in range(SPLIT):
                z_wait(0, c, h).wait_recv()

        @pl.when(q < last)
        def _():
            for h in range(SPLIT):
                z_wait(1, c, h).wait_recv()

        @pl.when(backward_edge)
        def _():
            for h in range(SPLIT):
                relay_copy(c, h).wait_send()

        def two_steps(pair_step, carry):
            for parity in range(2):
                t = 2 * pair_step + parity

                def advance(height, first, g):
                    base = first + height * g
                    level = [buf[parity, c, base - 1 + k] for k in range(height + 2)]
                    fresh = []
                    for k in range(height):
                        center = level[k + 1]
                        fresh.append(
                            coef[base + k, 0] * center
                            + coef[base + k, 1] * level[k + 2]
                            + coef[base + k, 2] * level[k]
                            + coef[base + k, 3] * pltpu.roll(center, lon - 1, 1)
                            + coef[base + k, 4] * pltpu.roll(center, 1, 1)
                        )
                    for k in range(height):
                        buf[1 - parity, c, base + k] = fresh[k]

                lax.fori_loop(0, (30 - 2 * t) // HEIGHT, lambda g, inner: (advance(HEIGHT, t + 1, g), inner)[1], 0)
                if HEIGHT == 4 and parity == 0:
                    advance(2, 29 - t, 0)
            return carry

        lax.fori_loop(0, STEPS // 2, two_steps, 0)
        for k in range(1, n_group):
            a_copy(0, c, *peer(k)).start()
        a_keep(0, c).start()
        if c < octs - 1:
            rest_start(c)

    for c in range(octs):
        a_keep(0, c).wait()
        for k in range(1, n_group):
            a_wait(0, c, *peer(k)).wait_recv()

    place = obs_index[...]
    n_obs = place.shape[1]
    hx = jnp.zeros((ens, n_obs), jnp.float32)
    inner = lax.broadcasted_iota(jnp.int32, (span, n_obs), 0) + start_at(m, 0)
    for row in range(rows):
        pick = jnp.where(inner + row * lon == place, 1.0, 0.0).astype(jnp.bfloat16)
        rest = fore[0, row]
        for _ in range(3):
            part = rest.astype(jnp.bfloat16)
            hx = hx + jnp.dot(part, pick, preferred_element_type=jnp.float32)
            rest = rest - part.astype(jnp.float32)
    column = place & (lon - 1)
    mine = (column >= start_at(m, 0)) & (column < start_at(m, 0) + span)
    ybar = jnp.sum(hx, axis=0, keepdims=True) / ens
    err = obs_var[...] * (1.0 + 2.0 * s.astype(jnp.float32) / float(n_slab - 1))
    anom = jnp.where(mine, (hx - ybar) / jnp.sqrt(err * (ens - 1.0)), 0.0)
    dev = (obs_values[...] - ybar) / jnp.sqrt(err)
    both = jnp.concatenate([anom, jnp.broadcast_to(dev, (ens, n_obs))], axis=0)
    high, low = halves(both)
    gpart[...] = lax.dot_general(
        left_parts(anom), jnp.concatenate([high, low, high], axis=1), (((1,), (1,)), ((), ())),
        preferred_element_type=jnp.float32,
    )

    def s_copy(other, ty, tm):
        return remote(
            gpart.at[pl.ds(pl.multiple_of(block * other, 8), block)], grecv.at[group],
            s_send.at[other], s_recv.at[group], device(q, ty, tm),
        )

    def s_wait(other, ty, tm):
        return remote(
            gpart.at[pl.ds(0, block)], grecv.at[other],
            s_send.at[other], s_recv.at[other], device(q, ty, tm),
        )

    for k in range(1, n_group):
        s_copy(*peer(k)).start()
    rest_start(octs - 1)
    grecv[group] = gpart[pl.ds(pl.multiple_of(block * group, 8), block)]
    for k in range(1, n_group):
        s_wait(*peer(k)).wait_recv()
    total = grecv[0]
    for k in range(1, n_group):
        total = total + grecv[k]
    gsum[...] = total

    def p_copy(k):
        tq = lax.rem(q + k, n_pair)
        return remote(gsum, precv.at[q], p_send.at[tq], p_recv.at[q], device(tq, y, m))

    def p_wait(k):
        tq = lax.rem(q + k, n_pair)
        return remote(gsum, precv.at[tq], p_send.at[tq], p_recv.at[tq], device(tq, y, m))

    for k in range(1, n_pair):
        p_copy(k).start()
    precv[q] = total
    for row in range(rows):
        ready[row] = right_parts(fore[0, row])
    for k in range(1, n_pair):
        p_wait(k).wait_recv()
    total = precv[0]
    for k in range(1, n_pair):
        total = total + precv[k]
    own = pl.ds(pl.multiple_of(block * group, 8), block)
    gfull[own] = total

    def g_copy(other, ty, tm):
        return remote(gfull.at[own], gfull.at[own], g_send.at[other], g_recv.at[group], device(q, ty, tm))

    def g_wait(other, ty, tm):
        rows_there = gfull.at[pl.ds(pl.multiple_of(block * other, 8), block)]
        return remote(rows_there, rows_there, g_send.at[other], g_recv.at[other], device(q, ty, tm))

    for k in range(1, n_group):
        g_copy(*peer(k)).start()
    for k in range(1, n_group):
        g_wait(*peer(k)).wait_recv()

    ident = jnp.where(
        lax.broadcasted_iota(jnp.int32, (ens, ens), 0) == lax.broadcasted_iota(jnp.int32, (ens, ens), 1), 1.0, 0.0
    )
    matrix = ident + gfull[:, :ens]
    scale = jnp.sum(jnp.sum(matrix * ident, axis=1, keepdims=True), axis=0, keepdims=True)

    upper = matrix / scale
    factor = 1.5 * ident - 0.5 * upper
    upper, lower = dot(upper, factor), factor
    for _ in range(ROOT_ITERATIONS - 1):
        factor = 1.5 * ident - 0.5 * dot(lower, upper)
        upper, lower = dot(upper, factor), dot(factor, lower)
    mean_w = dot(lower, dot(lower, gfull[:, ens:])) / (scale * jnp.sqrt(jnp.float32(ens - 1.0)))
    total_w = lower / jnp.sqrt(scale) + mean_w
    omega = 1.0 / ens + total_w - jnp.sum(total_w, axis=0, keepdims=True) / ens
    turned[...] = omega.T
    sibling = 2 * line + 1 - core
    weights = left_parts(
        jnp.concatenate(
            [turned[pl.ds(pl.multiple_of(kd * m, 8), kd)], turned[pl.ds(pl.multiple_of(kd * sibling, 8), kd)]], axis=0
        )
    )

    depth = rows // CHUNKS

    def b_copy(j, h):
        return remote(
            mixed.at[j, pl.ds(depth * h, depth)],
            out.at[pl.ds(depth * h, depth), :, pl.ds(start_at(m, j), span)],
            b_send.at[j, h], b_recv.at[j, h], device(q, y, sibling),
        )

    def b_wait(j, h):
        return remote(
            mixed.at[j, pl.ds(depth * h, depth)],
            out.at[pl.ds(depth * h, depth), :, pl.ds(start_at(sibling, j), span)],
            b_send.at[j, h], b_recv.at[j, h], device(q, y, sibling),
        )

    for j in range(n_line):
        if j > 0:
            for c in range(octs):
                a_keep(j, c).wait()
                for k in range(1, n_group):
                    a_wait(j, c, *peer(k)).wait_recv()
        for h in range(CHUNKS):
            for row in range(depth * h, depth * h + depth):
                result = product(weights, ready[row] if j == 0 else right_parts(fore[j, row]))
                mixed[j, row] = result[kd:]
                out[row, :, pl.ds(start_at(m, j), span)] = result[:kd]
            b_copy(j, h).start()

    for f in range(2):
        geo_pair(f).wait_send()
    for c in range(octs):
        for h in range(SPLIT):
            y_copy(c, h).wait_send()

    @pl.when(forward_edge)
    def _():
        for side in range(2):
            for f in range(2):
                geo_side(side, f).wait_send()
        for c in range(octs):
            for h in range(SPLIT):
                direct_copy(c, h).wait_send()

    for k in range(1, n_group):
        for c in range(octs):
            for j in range(n_line):
                a_copy(j, c, *peer(k)).wait_send()
        s_copy(*peer(k)).wait_send()
        g_copy(*peer(k)).wait_send()
    for k in range(1, n_pair):
        p_copy(k).wait_send()
    for j in range(n_line):
        for h in range(CHUNKS):
            b_copy(j, h).wait_send()
            b_wait(j, h).wait_recv()


def local(n_slab, n_mem, states, land_mask, cell_class, kappa, flow, obs_index, obs_values, obs_var):
    kd, rows, lon = states.shape
    ens = kd * n_mem
    n_pair, n_group, n_line, octs = n_slab // 2, 2 * n_mem, n_mem // 2, kd // 16
    span, block = lon // n_mem, ens // n_group
    n_obs = obs_index.shape[0]
    swapped = states.reshape(kd // 8, 8, rows, lon).transpose(0, 2, 1, 3)
    dma = pltpu.SemaphoreType.DMA
    vmem = pl.BlockSpec(memory_space=pltpu.VMEM)
    smem = pl.BlockSpec(memory_space=pltpu.SMEM)
    f32 = jnp.float32
    out = pl.pallas_call(
        functools.partial(cycle_kernel, n_slab, n_mem),
        out_shape=jax.ShapeDtypeStruct((rows, kd, lon), f32),
        in_specs=[vmem, vmem, vmem, smem, smem, vmem, vmem, vmem],
        out_specs=vmem,
        scratch_shapes=[
            pltpu.VMEM((2, octs, 4 * rows, 8, lon), f32),
            pltpu.VMEM((4 * rows, 5, 8, lon), f32),
            pltpu.VMEM((4, 2, rows, lon), jnp.int32),
            pltpu.VMEM((n_line, rows, ens, span), f32),
            pltpu.VMEM((n_line, rows, kd, span), f32),
            pltpu.VMEM((ens, 2 * ens), f32),
            pltpu.VMEM((n_group, block, 2 * ens), f32),
            pltpu.VMEM((block, 2 * ens), f32),
            pltpu.VMEM((n_pair, block, 2 * ens), f32),
            pltpu.VMEM((ens, 2 * ens), f32),
            pltpu.VMEM((ens, ens), f32),
            pltpu.VMEM((rows, 3 * ens, span), jnp.bfloat16),
            dma((3, 2)), dma((4, 2)), dma((octs, SPLIT)), dma((octs, SPLIT)), dma((octs, SPLIT)), dma((octs, SPLIT)),
            dma((2, octs, SPLIT)), dma((octs,)),
            dma((n_line, n_group, octs)), dma((n_line, n_group, octs)),
            dma((n_group,)), dma((n_group,)), dma((n_pair,)), dma((n_pair,)),
            dma((n_group,)), dma((n_group,)), dma((n_line, CHUNKS)), dma((n_line, CHUNKS)),
        ],
        compiler_params=pltpu.CompilerParams(
            collective_id=0, has_side_effects=True, vmem_limit_bytes=40 * 1024 * 1024
        ),
        name="cycle",
    )(
        swapped, cell_class, land_mask, kappa, flow,
        obs_index.reshape(1, n_obs), obs_values.reshape(1, n_obs), obs_var.reshape(1, n_obs),
    )
    return out.transpose(1, 0, 2)


def solution(mesh):
    return jax.shard_map(
        functools.partial(local, mesh.shape["slab"], mesh.shape["mem"]),
        mesh=mesh,
        in_specs=(
            P("mem", "slab", None),
            P("slab", None),
            P("slab", None),
            P(),
            P(),
            P("slab"),
            P("slab"),
            P("slab"),
        ),
        out_specs=P("mem", "slab", None),
        check_vma=False,
    )
```
